32 devices in a mesh: scene: 2 (over y), rows: 4 (over z), cols: 2 (over x), chan: 2 (over core).
Axes of the slice: x: 2, y: 2, z: 4, core: 2. Of those that a mesh axis runs over, the one named last changes fastest.
Arguments:
- position: float32 [3, 4096], P(None, ('scene', 'rows', 'cols', 'chan')), parts along dimension 1, may hold values from 0 to 1
- tilt: float32 [2, 4096], P(None, ('scene', 'rows', 'cols', 'chan')), parts along dimension 1, may hold values from -3.140625 to 3.140625
- patch_area: float32 [4096], P(('scene', 'rows', 'cols', 'chan')), parts along dimension 0, may hold values from 0.005859375 to 0.0234375
- reflect: float32 [3, 4096], P(None, ('scene', 'rows', 'cols', 'chan')), parts along dimension 1, may hold values from 0.2 to 0.9
- emission: float32 [96, 4096], P(None, ('scene', 'rows', 'cols', 'chan')), parts along dimension 1, may hold values from 0.05 to 1
- radiosity: bfloat16 [96, 4096], P(None, ('scene', 'rows', 'cols', 'chan')), parts along dimension 1, may hold values from 0.25 to 2
- cotangent: bfloat16 [96, 4096], P(None, ('scene', 'rows', 'cols', 'chan')), parts along dimension 1, may hold values from -0.5 to 1.5
- block_inverse: bfloat16 [8, 512, 512], P(('scene', 'rows')), parts along dimension 0, may hold values from -1 to 2
- visibility: int32 [32, 16], P('scene'), parts along dimension 0, may hold values from 0 to 1
- cluster_ids: int32 [8], P('scene'), parts along dimension 0, may hold values from 0 to 3, each once
Outputs:
- radiosity_next: bfloat16 [96, 4096], P(None, ('scene', 'rows', 'cols', 'chan')), parts along dimension 1
- gradient: float32 [96, 4096], P(None, ('scene', 'rows', 'cols', 'chan')), parts along dimension 1
The draws below stay inside these ranges and needn't reach their ends.
There are 2 independent parts, one for each index of `scene`. The reference program is written for one: setup_inputs(seed, part) draws one part's arguments, and reference() takes and returns one part's arrays. A program takes and returns all parts, laid end to end along the dimension named above; each array names one. Nothing has to cross between parts.
All inputs are finite; a program needn't handle non-finite values.
Results may differ from the reference program's by a relative error of at most 0.0095.
Values may be sent and summed in bfloat16 or wider, within the bound.
No kernel may reach another device: no remote copies, remote signals or barrier semaphores. Data moves between devices by JAX's collectives and lax.ppermute only.
A program may use at most 64 MiB of HBM per device.

```python
import math
import jax
import jax.numpy as jnp
from jax import lax

CLUSTER = 512
SUB = 128
LIGHTS = 32
CHANNELS = 96
PATCHES = 2048
CLUSTERS = 4
BLOCKS = 16


def draw_block_inverse(key, part):
    shape = (CLUSTERS, CLUSTER, CLUSTER)
    noise = jax.random.normal(key, shape, jnp.float32)
    identity = jnp.eye(CLUSTER, dtype=jnp.float32)
    return (identity[None] + 0.35 * jnp.clip(noise, -4.0, 4.0) * CLUSTER ** (-0.5)).astype(jnp.bfloat16)


def draw_visibility(key, part):
    keys = jax.random.split(jax.random.fold_in(key, 11), 3)
    openness = jax.random.randint(keys[0], (BLOCKS,), 4, 17)
    rolls_recv = jax.random.randint(keys[1], (BLOCKS, BLOCKS), 0, 16)
    rolls_src = jax.random.randint(keys[2], (BLOCKS, BLOCKS), 0, 16)
    seen = (rolls_recv < openness[:, None]) & (rolls_src < openness[None, :])
    return seen.astype(jnp.int32)


def shard_levels(key, shape, shards, least, largest):
    level, own = 1.0, jax.random.fold_in(key, 6)
    for dim, shards_of in shards:
        steps = jnp.exp(jax.random.uniform(jax.random.fold_in(own, dim), (shards_of,), jnp.float32, least / len(shards), largest / len(shards)))
        level = level * jnp.repeat(steps, shape[dim] // shards_of).reshape([-1 if axis == dim else 1 for axis in range(len(shape))])
    return level


def setup_inputs(seed: int = 0, part: int = 0) -> dict:
    key_list = jax.random.split(jax.random.key(seed), 11)
    part_splits = jax.random.split(jax.random.fold_in(key_list[10], part), 11)
    return {
        "position": jnp.clip(1.0 * jax.random.uniform(part_splits[0], (3, PATCHES), jnp.float32) ** shard_levels(part_splits[0], (3, PATCHES), ((1, 16),), -0.2, 0.2), 0.0, 1.0),
        "tilt": jnp.clip(jax.random.uniform(part_splits[1], (2, PATCHES), jnp.float32, -3.140625, 3.140625), -3.140625, 3.140625),
        "patch_area": jnp.clip(jnp.exp(math.log(0.0234375) - 1.3862944 * jax.random.uniform(part_splits[2], (PATCHES,), jnp.float32) ** shard_levels(part_splits[2], (PATCHES,), ((0, 16),), -0.2, 0.2)), 0.005859375, 0.0234375),
        "reflect": jnp.clip(0.2 + 0.7 * jax.random.uniform(part_splits[3], (3, PATCHES), jnp.float32) ** shard_levels(part_splits[3], (3, PATCHES), ((1, 16),), -0.2, 0.2), 0.2, 0.9),
        "emission": jnp.clip(jnp.exp(math.log(1.0) - 2.9957323 * jax.random.uniform(part_splits[4], (CHANNELS, PATCHES), jnp.float32) ** shard_levels(part_splits[4], (CHANNELS, PATCHES), ((1, 16),), -0.2, 0.2)), 0.05, 1.0),
        "radiosity": jnp.clip(jnp.exp(math.log(2.0) - 2.0794415 * jax.random.uniform(part_splits[5], (CHANNELS, PATCHES), jnp.float32) ** shard_levels(part_splits[5], (CHANNELS, PATCHES), ((1, 16),), -0.2, 0.2)), 0.25, 2.0).astype(jnp.bfloat16),
        "cotangent": jnp.clip(-0.5 + 2.0 * jax.random.uniform(part_splits[6], (CHANNELS, PATCHES), jnp.float32) ** shard_levels(part_splits[6], (CHANNELS, PATCHES), ((1, 16),), -0.2, 0.2), -0.5, 1.5).astype(jnp.bfloat16),
        "block_inverse": draw_block_inverse(jax.random.fold_in(jax.random.fold_in(key_list[10], part), 71), part),
        "visibility": draw_visibility(jax.random.fold_in(jax.random.fold_in(key_list[10], part), 71), part),
        "cluster_ids": jax.random.permutation(part_splits[9], CLUSTERS).astype(jnp.int32),
    }


def normals(tilt):
    a = tilt[0]
    b = tilt[1]
    return jnp.stack([jnp.cos(a) * jnp.cos(b), jnp.sin(a) * jnp.cos(b), jnp.sin(b)])


def factors(recv_pos, recv_normal, src_pos, src_normal, src_area, visible):
    offset_vec = src_pos[:, None, :] - recv_pos[:, :, None]
    distance = jnp.sum(offset_vec * offset_vec, axis=0)
    facing = jnp.sum(recv_normal[:, :, None] * offset_vec, axis=0)
    behind = -jnp.sum(src_normal[:, None, :] * offset_vec, axis=0)
    spread = distance + src_area[None, :]
    value = jnp.maximum(facing, 0.0) * jnp.maximum(behind, 0.0) * src_area[None, :] / (jnp.pi * spread * spread)
    return (value * visible).astype(jnp.bfloat16)


def reference(position, tilt, patch_area, reflect, emission, radiosity, cotangent, block_inverse, visibility, cluster_ids):
    normal = normals(tilt)
    sub_count = CLUSTER // SUB
    indices = jnp.arange(PATCHES, dtype=jnp.int32)
    slot_cluster = indices // CLUSTER
    block_id = jnp.take(cluster_ids, slot_cluster) * sub_count + (indices % CLUSTER) // SUB
    rho_all = jnp.tile(reflect, (LIGHTS, 1))

    def sweep_step(gradient, index):
        start = index * CLUSTER
        recv_pos = lax.dynamic_slice_in_dim(position, start, CLUSTER, 1)
        recv_normal = lax.dynamic_slice_in_dim(normal, start, CLUSTER, 1)
        recv_block = cluster_ids[index] * sub_count + jnp.arange(sub_count, dtype=jnp.int32)
        visible_sub = jnp.take(jnp.take(visibility, recv_block, axis=0), block_id, axis=1).astype(jnp.float32)
        visible_sub = visible_sub * (slot_cluster != index).astype(jnp.float32)[None, :]
        visible = jnp.repeat(visible_sub, SUB, axis=0)
        factor_tile = factors(recv_pos, recv_normal, position, normal, patch_area, visible)
        gathered = jnp.dot(radiosity, factor_tile.T, preferred_element_type=jnp.float32)
        inverse_half = block_inverse[index]
        inverse = inverse_half.astype(jnp.float32)
        rho_here = lax.dynamic_slice_in_dim(rho_all, start, CLUSTER, 1)
        terms = lax.dynamic_slice_in_dim(emission, start, CLUSTER, 1) + rho_here * gathered
        solved = jnp.dot(terms, inverse.T, precision=lax.Precision.HIGHEST)
        cot_here = lax.dynamic_slice_in_dim(cotangent, start, CLUSTER, 1)
        adjoint = jnp.dot(cot_here, inverse_half, preferred_element_type=jnp.float32)
        weight = (rho_here * adjoint).astype(jnp.bfloat16)
        gradient = gradient + jnp.dot(weight, factor_tile, preferred_element_type=jnp.float32)
        return gradient, solved.astype(jnp.bfloat16)

    gradient, pieces = lax.scan(sweep_step, jnp.zeros((CHANNELS, PATCHES), jnp.float32), jnp.arange(CLUSTERS, dtype=jnp.int32))
    radiosity_next = jnp.transpose(pieces, (1, 0, 2)).reshape(CHANNELS, PATCHES)
    return radiosity_next, gradient
```

```python
import jax
import jax.numpy as jnp
from jax import lax
from jax.experimental import pallas as pl
from jax.experimental.pallas import tpu as pltpu
from jax.sharding import PartitionSpec as P

CLUSTER = 512
SUB = 128
SUBS = CLUSTER // SUB
COLORS = 3
LANES = 128
GEO = 32
Q_ROWS = 9
Z_ROWS = 8

AXES = ("scene", "rows", "cols", "chan")
VMEM = pl.BlockSpec(memory_space=pltpu.VMEM)
SMEM = pl.BlockSpec(memory_space=pltpu.SMEM)


def parity(bits):
    return bin(bits).count("1") % 2


def doubling_steps(size):
    if size & (size - 1):
        raise ValueError("axis size")
    return [2 << k | 1 for k in range(size.bit_length() - 1)]


def repeat(count, body):
    if count <= 4:
        for i in range(count):
            body(i)
    else:
        lax.fori_loop(0, count, lambda i, unused: (body(i), unused)[1], 0)


def swap(values, axes, size, mask):
    return lax.ppermute(values, axes, [(i, i ^ mask) for i in range(size)])


def row_block(index):
    col = lax.axis_index("cols") ^ (index >> 1)
    chan = lax.axis_index("chan") ^ ((index & 1) ^ parity(index >> 1))
    return col * 2 + chan


def three_parts(values):
    upper = values.astype(jnp.bfloat16)
    rest = values - upper.astype(jnp.float32)
    middle = rest.astype(jnp.bfloat16)
    lower = rest - middle.astype(jnp.float32)
    return upper.astype(jnp.float32), middle.astype(jnp.float32), lower


def pack_kernel(pos_ref, tilt_ref, area_ref, reflect_ref, rad_ref, cot_ref, z_ref, q_ref, geo):
    channels = rad_ref.shape[0]
    a = tilt_ref[0:1, :]
    b = tilt_ref[1:2, :]
    geo[...] = jnp.zeros_like(geo)
    geo[0:3, :] = pos_ref[...]
    geo[3:4, :] = jnp.cos(a) * jnp.cos(b)
    geo[4:5, :] = jnp.sin(a) * jnp.cos(b)
    geo[5:6, :] = jnp.sin(b)
    geo[6:7, :] = area_ref[...]
    parts = three_parts(geo[0:8, :])
    z_ref[0:channels, :] = rad_ref[...]
    packed = jnp.concatenate([*parts, jnp.zeros_like(parts[0])], axis=0)
    z_ref[channels:, :] = packed.astype(jnp.bfloat16)
    geo[6:9, :] = reflect_ref[...]
    parts = three_parts(geo[0:16, :])
    for k in range(3):
        geo[k * Q_ROWS : (k + 1) * Q_ROWS, :] = parts[k][0:Q_ROWS, :]
    q_ref[0:channels, :] = cot_ref[...]
    q_ref[channels:, :] = geo[...].astype(jnp.bfloat16)


def visible_kernel(blocks, subs, vis_ref, ids_ref, keep_ref):
    row = lax.axis_index("rows")
    col = lax.axis_index("cols")
    chan = lax.axis_index("chan")
    first = row * (subs * SUB // CLUSTER)
    for b in range(blocks):
        slot = (row ^ b) * subs + col * 2 + (chan ^ parity(b))
        src_cluster = slot // SUBS
        src_block = ids_ref[src_cluster] * SUBS + lax.rem(slot, SUBS)
        for t in range(subs):
            recv_cluster = first + t // SUBS
            seen = vis_ref[ids_ref[recv_cluster] * SUBS + t % SUBS, src_block]
            seen = jnp.where(recv_cluster != src_cluster, seen, 0)
            keep_ref[b * subs + t : b * subs + t + 1, :] = jnp.full((1, LANES), seen.astype(jnp.float32))


def spread_rows(rows, targets):
    part = lax.broadcasted_iota(jnp.int32, (GEO, targets), 0)
    hit = (part == rows) | (part == rows + Q_ROWS) | (part == rows + 2 * Q_ROWS)
    return hit.astype(jnp.float32).astype(jnp.bfloat16)


def factor_tile(block_ref, start, channels, keep_ref, keep_row, geo_ref, tile_ref, lane):
    parts = block_ref[pl.ds(start + channels, GEO), :].astype(jnp.float32)
    src = parts[0:8, :] + parts[8:16, :] + parts[16:24, :]
    area = src[6:7, :]

    def receivers(t):
        at = pl.ds(t * SUB, SUB)
        v = [src[k : k + 1, :] - geo_ref[k, at, :] for k in range(3)]
        distance = v[0] * v[0] + v[1] * v[1] + v[2] * v[2]
        facing = geo_ref[3, at, :] * v[0] + geo_ref[4, at, :] * v[1] + geo_ref[5, at, :] * v[2]
        behind = -(src[3:4, :] * v[0] + src[4:5, :] * v[1] + src[5:6, :] * v[2])
        spread = distance + area
        scale = area * keep_ref[pl.ds(keep_row + t, 1), :]
        value = jnp.maximum(facing, 0.0) * jnp.maximum(behind, 0.0) * scale / (jnp.pi * spread * spread)
        tile_ref[at, pl.ds(lane * SUB, SUB)] = value.astype(jnp.bfloat16)

    repeat(tile_ref.shape[0] // SUB, receivers)


ROW_BY_ROW = (((1,), (1,)), ((), ()))


def dot(a, b, dims=(((1,), (0,)), ((), ()))):
    return lax.dot_general(a, b, dims, preferred_element_type=jnp.float32)


def sources(blocks, first, block_ref, keep_ref, geo_ref, weight_ref, tile_ref):
    channels, receivers = weight_ref.shape
    height = channels + GEO
    subs = receivers // SUB
    repeat(
        blocks,
        lambda i: factor_tile(block_ref, i * height, channels, keep_ref, (first + i) * subs, geo_ref, tile_ref, i),
    )
    tile = tile_ref[...]
    rad = jnp.concatenate([block_ref[i * height : i * height + channels, :] for i in range(blocks)], axis=1)
    return dot(rad, tile, ROW_BY_ROW), dot(weight_ref[...], tile)


def early_kernel(
    near_ref, far_ref, src_ref, keep_ref, inv_ref, weight_ref, geo_ref, rho_ref, fwd_ref, grad_ref, cot_ref, tile_ref
):
    channels, receivers = weight_ref.shape
    height = channels + GEO
    half = near_ref.shape[0] // height
    color = lax.rem(lax.broadcasted_iota(jnp.int32, (GEO, channels), 1), COLORS)
    pick_rho = spread_rows(6 + color, channels)
    for b in range(2 * half):
        ref, at = (near_ref, b) if b < half else (far_ref, b - half)
        lanes = pl.ds(pl.multiple_of(row_block(b) * SUB, SUB), SUB)
        cot_ref[:, lanes] = ref[at * height : at * height + channels, :]
        parts = ref[at * height + channels : (at + 1) * height, :]
        rho_ref[:, lanes] = dot(pick_rho, parts, (((0,), (0,)), ((), ())))
        for k in range(6):
            geo_ref[k, lanes, :] = dot(parts, spread_rows(k, LANES), (((0,), (0,)), ((), ())))
    for k in range(receivers // CLUSTER):
        at = slice(k * CLUSTER, (k + 1) * CLUSTER)
        weight_ref[:, at] = (rho_ref[:, at] * dot(cot_ref[:, at], inv_ref[k])).astype(jnp.bfloat16)
    blocks = grad_ref.shape[0] // channels
    fwd, grad = sources(blocks, 0, src_ref, keep_ref, geo_ref, weight_ref, tile_ref)
    fwd_ref[...] = fwd
    for i in range(blocks):
        grad_ref[i * channels : (i + 1) * channels, :] = grad[:, i * SUB : (i + 1) * SUB]


def late_kernel(
    src_ref,
    keep_ref,
    inv_ref,
    weight_ref,
    geo_ref,
    rho_ref,
    fwd_ref,
    emission_ref,
    grad_ref,
    near_ref,
    far_ref,
    terms_ref,
    solved_ref,
    tile_ref,
):
    channels, receivers = weight_ref.shape
    blocks = grad_ref.shape[0] // channels
    fwd, grad = sources(blocks, blocks, src_ref, keep_ref, geo_ref, weight_ref, tile_ref)
    for i in range(blocks):
        grad_ref[i * channels : (i + 1) * channels, :] = grad[:, i * SUB : (i + 1) * SUB].astype(jnp.bfloat16)
    terms_ref[...] = rho_ref[...] * (fwd_ref[...] + fwd)
    own = pl.ds(pl.multiple_of(row_block(0) * SUB, SUB), SUB)
    terms_ref[:, own] = terms_ref[:, own] + emission_ref[...]
    for k in range(receivers // CLUSTER):
        at = slice(k * CLUSTER, (k + 1) * CLUSTER)
        terms = terms_ref[:, at]
        upper = terms.astype(jnp.bfloat16)
        lower = (terms - upper.astype(jnp.float32)).astype(jnp.bfloat16)
        solved_ref[:, at] = dot(upper, inv_ref[k], ROW_BY_ROW) + dot(lower, inv_ref[k], ROW_BY_ROW)
    half = near_ref.shape[0] // channels
    for b in range(2 * half):
        lanes = pl.ds(pl.multiple_of(row_block(b) * SUB, SUB), SUB)
        if b < half:
            near_ref[b * channels : (b + 1) * channels, :] = solved_ref[:, lanes]
        else:
            far_ref[(b - half) * channels : (b - half + 1) * channels, :] = solved_ref[:, lanes].astype(jnp.bfloat16)


def halving(kept, sent, axes, size, masks):
    while True:
        kept = kept + swap(sent, axes, size, masks[-1]).astype(jnp.float32)
        masks = masks[:-1]
        if not masks:
            return kept
        half = kept.shape[0] // 2
        kept, sent = kept[:half], kept[half:].astype(jnp.bfloat16)


def local(
    position, tilt, patch_area, reflect, emission, radiosity, cotangent, block_inverse, visibility, cluster_ids
):
    channels, dev_patches = radiosity.shape
    rows, cols, chan = (lax.axis_size(name) for name in ("rows", "cols", "chan"))
    if dev_patches != SUB or chan != 2 or rows < 2 or cols < 2:
        raise ValueError("split")
    subs = cols * chan
    receivers = subs * SUB
    height = channels + GEO
    f32, bf16 = jnp.float32, jnp.bfloat16
    q_axes, q_masks = ("cols", "chan"), [1, *doubling_steps(cols)]
    z_axes, z_masks = ("rows", "chan"), doubling_steps(rows)

    z_block, q_block = pl.pallas_call(
        pack_kernel,
        out_shape=[jax.ShapeDtypeStruct((height, SUB), bf16)] * 2,
        in_specs=[VMEM] * 6,
        out_specs=[VMEM] * 2,
        scratch_shapes=[pltpu.VMEM((GEO, SUB), f32)],
        name="pack",
    )(position, tilt, patch_area[None, :], reflect, radiosity, cotangent)

    keep = pl.pallas_call(
        lambda *refs: visible_kernel(rows, subs, *refs),
        out_shape=jax.ShapeDtypeStruct((rows * subs, LANES), f32),
        in_specs=[SMEM] * 2,
        out_specs=VMEM,
        name="visible",
    )(visibility, cluster_ids)

    q_near, z_near = q_block, z_block
    for mask in q_masks[:-1]:
        q_near = jnp.concatenate([q_near, swap(q_near, q_axes, subs, mask)], axis=0)
    for mask in z_masks[:-1]:
        z_near = jnp.concatenate([z_near, swap(z_near, z_axes, rows * chan, mask)], axis=0)
    q_far = swap(q_near, q_axes, subs, q_masks[-1])
    z_far = swap(z_near, z_axes, rows * chan, z_masks[-1])

    blocks = rows // 2
    weight, geo, rho, fwd, grad_near = pl.pallas_call(
        early_kernel,
        out_shape=[
            jax.ShapeDtypeStruct((channels, receivers), bf16),
            jax.ShapeDtypeStruct((6, receivers, LANES), f32),
            jax.ShapeDtypeStruct((channels, receivers), f32),
            jax.ShapeDtypeStruct((channels, receivers), f32),
            jax.ShapeDtypeStruct((blocks * channels, SUB), f32),
        ],
        in_specs=[VMEM] * 5,
        out_specs=[VMEM] * 5,
        scratch_shapes=[pltpu.VMEM((channels, receivers), bf16), pltpu.VMEM((receivers, blocks * SUB), bf16)],
        name="early",
    )(q_near, q_far, z_near, keep, block_inverse)

    grad_far, solved_near, solved_far = pl.pallas_call(
        late_kernel,
        out_shape=[
            jax.ShapeDtypeStruct((blocks * channels, SUB), bf16),
            jax.ShapeDtypeStruct((subs // 2 * channels, SUB), f32),
            jax.ShapeDtypeStruct((subs // 2 * channels, SUB), bf16),
        ],
        in_specs=[VMEM] * 8,
        out_specs=[VMEM] * 3,
        scratch_shapes=[
            pltpu.VMEM((channels, receivers), f32),
            pltpu.VMEM((channels, receivers), f32),
            pltpu.VMEM((receivers, blocks * SUB), bf16),
        ],
        name="late",
    )(z_far, keep, block_inverse, weight, geo, rho, fwd, emission)

    gradient = halving(grad_near, grad_far, z_axes, rows * chan, z_masks)
    solved = halving(solved_near, solved_far, q_axes, subs, q_masks)
    return solved.astype(bf16), gradient


def solution(mesh):
    split = P(None, AXES)
    return jax.shard_map(
        local,
        mesh=mesh,
        in_specs=(
            split,
            split,
            P(AXES),
            split,
            split,
            split,
            split,
            P(("scene", "rows"), None, None),
            P("scene", None),
            P("scene"),
        ),
        out_specs=(split, split),
        check_vma=False,
    )
```
